32 devices in a mesh: samp: 8 (over z, y), feat: 4 (over x, core).
Axes of the slice: x: 2, y: 2, z: 4, core: 2. Of those that a mesh axis runs over, the one named last changes fastest.
Arguments:
- data: bfloat16 [8192, 4096], P('samp', 'feat'), may hold values from -0.09375 to 0.09375
- targets: float32 [8192, 256], P('samp'), may hold values from -24 to 24
- tile_x: float32 [8, 4096, 256], P('samp', 'feat'), may hold values from -6 to 6
- x_dual: float32 [8, 4096, 256], P('samp', 'feat'), may hold values from -6 to 6
- tile_y: float32 [4, 8192, 256], P('feat', 'samp'), may hold values from -6 to 6
- y_dual: float32 [4, 8192, 256], P('feat', 'samp'), may hold values from -6 to 6
Outputs:
- new_x: float32 [8, 4096, 256], P('samp', 'feat')
- new_x_dual: float32 [8, 4096, 256], P('samp', 'feat')
- new_y: float32 [4, 8192, 256], P('feat', 'samp')
- new_y_dual: float32 [4, 8192, 256], P('feat', 'samp')
The draws below stay inside these ranges and needn't reach their ends.
All inputs are finite; a program needn't handle non-finite values.
Results may differ from the reference program's by a relative error of at most 0.0041.
Values sent between devices are 32-bit elements; how exact they have to be, the bound alone decides.
A program may use at most 128 MiB of HBM per device.

```python
import jax
import jax.numpy as jnp
from jax import lax

TILE_ROWS = 1024
TILE_COLS = 1024
TARGETS = 256
ITERS = 2
SAMPLES = 8192
FEATURES = 4096
SAMP_BLOCKS = 8
FEAT_BLOCKS = 4
N_SAMP = 8
N_FEAT = 4


def level_of(stream_key, extent, pieces, least, largest):
    level, own = 1.0, jax.random.fold_in(stream_key, 6)
    for position, blocks in pieces:
        heights = jnp.exp(jax.random.uniform(jax.random.fold_in(own, position), (blocks,), jnp.float32, least / len(pieces), largest / len(pieces)))
        level = level * jnp.repeat(heights, extent[position] // blocks).reshape([-1 if axis == position else 1 for axis in range(len(extent))])
    return level


def gaussian(rng, dims, deviation, bound, split=(), kind=jnp.bfloat16):
    drawn = deviation * jax.random.normal(rng, dims, jnp.float32)
    if split:
        drawn = drawn * level_of(rng, dims, split, -0.22, 0.18)
    return jnp.clip(drawn, -bound, bound).astype(kind)


def setup_inputs(seed: int = 0) -> dict:
    keys = jax.random.split(jax.random.key(seed), 7)
    return {
        "data": gaussian(keys[0], (SAMPLES, FEATURES), (4 * TILE_COLS) ** -0.5, 0.09375, ((0, 8), (1, 4))),
        "targets": gaussian(keys[1], (SAMPLES, TARGETS), 4.0, 24.0, ((0, 8),), jnp.float32),
        "tile_x": gaussian(keys[2], (SAMP_BLOCKS, FEATURES, TARGETS), 1.0, 6.0, ((0, 8), (1, 4)), jnp.float32),
        "x_dual": gaussian(keys[3], (SAMP_BLOCKS, FEATURES, TARGETS), 1.0, 6.0, ((0, 8), (1, 4)), jnp.float32),
        "tile_y": gaussian(keys[4], (FEAT_BLOCKS, SAMPLES, TARGETS), 1.0, 6.0, ((0, 4), (1, 8)), jnp.float32),
        "y_dual": gaussian(keys[5], (FEAT_BLOCKS, SAMPLES, TARGETS), 1.0, 6.0, ((0, 4), (1, 8)), jnp.float32),
    }


huber_width = 0.5
shrink_level = 0.1
highest = lax.Precision.HIGHEST


def soft_shrink(values):
    return jnp.sign(values) * jnp.maximum(jnp.abs(values) - shrink_level, 0.0)


def huber_prox(values, weight):
    limit = huber_width * (1.0 + weight)
    return jnp.where(jnp.abs(values) <= limit, values / (1.0 + weight), values - weight * huber_width * jnp.sign(values))


def inverse_of(matrix):
    gram = lax.dot_general(matrix, matrix, (((1,), (1,)), ((), ())), preferred_element_type=jnp.float32)
    order = matrix.shape[0]
    identity = jnp.eye(order, dtype=jnp.float32)
    system = identity + gram
    factor = 1.0 / (1.0 + 2.0 * jnp.trace(gram) / order)
    first = 2.0 * factor * identity - factor * factor * system
    product = jnp.dot(system, first, precision=highest)
    inverse = jnp.dot(first, 2.0 * identity - product, precision=highest)
    return system, inverse


def project(operands):
    matrix, start, aim = operands
    system, inverse = inverse_of(matrix)
    rounded_start = start.astype(jnp.bfloat16)
    residual = jnp.dot(matrix, rounded_start, preferred_element_type=jnp.float32) - aim
    weights = jnp.dot(inverse, residual, precision=highest)
    rounded_weights = weights.astype(jnp.bfloat16)
    back = lax.dot_general(matrix, rounded_weights, (((0,), (0,)), ((), ())), preferred_element_type=jnp.float32)
    new_x = start - back
    new_y = residual + aim - jnp.dot(system, weights, precision=highest) + weights
    return new_x, new_y


def reference(data, targets, tile_x, x_dual, tile_y, y_dual):
    n_samp = N_SAMP
    n_feat = N_FEAT
    tiles = data.reshape(n_samp, TILE_ROWS, n_feat, TILE_COLS).transpose(0, 2, 1, 3).reshape(n_samp * n_feat, TILE_ROWS, TILE_COLS)
    coeffs, coeff_dual, partials, partial_dual = tile_x, x_dual, tile_y, y_dual
    for turn_index in range(ITERS):
        consensus = soft_shrink(jnp.sum(coeffs + coeff_dual, axis=0) / n_samp)
        joined = partials + partial_dual
        total = jnp.sum(joined, axis=0)
        fitted = targets + huber_prox(total - targets, float(n_feat))
        exchanged = joined + (fitted - total) / n_feat
        coeff_dual = coeff_dual + coeffs - consensus[None]
        partial_dual = partial_dual + partials - exchanged
        start = consensus[None] - coeff_dual
        aim = exchanged - partial_dual
        start_tiles = start.reshape(n_samp * n_feat, TILE_COLS, TARGETS)
        aim_tiles = aim.reshape(n_feat, n_samp, TILE_ROWS, TARGETS).transpose(1, 0, 2, 3).reshape(n_samp * n_feat, TILE_ROWS, TARGETS)
        new_x, new_y = lax.map(project, (tiles, start_tiles, aim_tiles))
        coeffs = new_x.reshape(n_samp, n_feat * TILE_COLS, TARGETS)
        partials = new_y.reshape(n_samp, n_feat, TILE_ROWS, TARGETS).transpose(1, 0, 2, 3).reshape(n_feat, n_samp * TILE_ROWS, TARGETS)
    return coeffs, coeff_dual, partials, partial_dual
```

```python
import jax
import jax.numpy as jnp
from jax import lax
from jax.sharding import PartitionSpec as P

ITERS = 2
huber_width = 0.5
shrink_level = 0.1
f32 = jnp.float32
bf16 = jnp.bfloat16


def soft_shrink(values):
    return jnp.sign(values) * jnp.maximum(jnp.abs(values) - shrink_level, 0.0)


def huber_prox(values, weight):
    limit = huber_width * (1.0 + weight)
    return jnp.where(
        jnp.abs(values) <= limit,
        values / (1.0 + weight),
        values - weight * huber_width * jnp.sign(values),
    )


def dot(a, b):
    return jnp.dot(a, b, preferred_element_type=f32)


def shards(data, targets, tile_x, x_dual, tile_y, y_dual):
    n_samp = lax.axis_size("samp")
    n_feat = lax.axis_size("feat")
    order = data.shape[0]
    q = tile_x[0] + x_dual[0]
    p = tile_y[0] + y_dual[0]
    gram = lax.dot_general(data, data, (((1,), (1,)), ((), ())), preferred_element_type=f32)
    identity = jnp.eye(order, dtype=f32)
    wide = data.astype(f32)
    factor = 1.0 / (1.0 + 2.0 * jnp.sum(wide * wide) / order)
    a = 2.0 * factor - factor * factor
    b = factor * factor
    g16 = gram.astype(bf16)
    inner = (2.0 - a) * identity + (b - a) * gram + b * dot(g16, g16)
    inverse = a * inner - b * dot(g16, inner.astype(bf16))
    back_map = lax.dot_general(
        data, inverse.astype(bf16), (((0,), (0,)), ((), ())), preferred_element_type=f32
    ).astype(bf16)
    for turn_index in range(ITERS):
        consensus = soft_shrink(lax.psum(q, "samp") / n_samp)
        total = lax.psum(p, "feat")
        correction = (targets + huber_prox(total - targets, float(n_feat)) - total) / n_feat
        dual = q - consensus
        start = consensus - dual
        aim = p + 2.0 * correction
        ahead = dot(data, start.astype(bf16))
        back = dot(back_map, (ahead - aim).astype(bf16))
        coeffs = start - back
        partials = ahead - dot(data, back.astype(bf16))
        q = consensus - back
        p = partials - correction
    return (coeffs[None], dual[None], partials[None], -correction[None])


def solution(mesh):
    return jax.shard_map(
        shards,
        mesh=mesh,
        in_specs=(
            P("samp", "feat"),
            P("samp", None),
            P("samp", "feat", None),
            P("samp", "feat", None),
            P("feat", "samp", None),
            P("feat", "samp", None),
        ),
        out_specs=(
            P("samp", "feat", None),
            P("samp", "feat", None),
            P("feat", "samp", None),
            P("feat", "samp", None),
        ),
        check_vma=False,
    )
```

```python
import jax
import jax.numpy as jnp
from jax import lax
from jax.experimental import pallas as pl
from jax.experimental.pallas import tpu as pltpu
from jax.sharding import PartitionSpec as P

ITERS = 2
LANES = 128
BLOCK = 256
HALVES = 2
huber_width = 0.5
shrink_level = 0.1
f32 = jnp.float32
bf16 = jnp.bfloat16


def dot(a, b):
    return jnp.dot(a, b, preferred_element_type=f32)


def split(value):
    high = value.astype(bf16)
    low = (value - high.astype(f32)).astype(bf16)
    return jnp.concatenate([high, low], axis=1)


def joined_halves(value):
    return value[:, :LANES] + value[:, LANES:]


def soft_shrink(values):
    return values - jnp.clip(values, -shrink_level, shrink_level)


def huber_prox(values, weight):
    limit = huber_width * (1.0 + weight)
    shift = jnp.where(values > 0.0, weight * huber_width, -weight * huber_width)
    return jnp.where(jnp.abs(values) <= limit, values * (1.0 / (1.0 + weight)), values - shift)


def all_reduce(buf, rec, out, send, recv, axis, order, base, rows):
    index = lax.axis_index(axis)
    off, length, at, slot = base, rows, base, 0
    path = []
    for k, bit in enumerate(order):
        side = (index // (1 << bit)) % 2
        peer = index + (1 - 2 * side) * (1 << bit)
        if k < len(order) - 1:
            half = length // 2
            keep = off + side * half
            give = off + (1 - side) * half
            path.append((peer, off, length))
        else:
            half, keep, give = length, off, off
        if not isinstance(keep, int):
            keep, give = pl.multiple_of(keep, 8), pl.multiple_of(give, 8)
        copy = pltpu.make_async_remote_copy(
            src_ref=buf.at[pl.ds(give, half)],
            dst_ref=rec.at[pl.ds(at, half)],
            send_sem=send.at[slot],
            recv_sem=recv.at[slot],
            device_id={axis: peer},
            device_id_type=pl.DeviceIdType.MESH,
        )
        copy.start()
        yield
        copy.wait()
        target = buf if k < len(order) - 1 else out
        target[pl.ds(keep, half)] = buf[pl.ds(keep, half)] + rec[pl.ds(at, half)]
        off, length, at, slot = keep, half, at + half, slot + 1
    for peer, parent, extent in reversed(path):
        copy = pltpu.make_async_remote_copy(
            src_ref=out.at[pl.ds(off, length)],
            dst_ref=out.at[pl.ds(off, length)],
            send_sem=send.at[slot],
            recv_sem=recv.at[slot],
            device_id={axis: peer},
            device_id_type=pl.DeviceIdType.MESH,
        )
        copy.start()
        yield
        copy.wait()
        off, length, slot = parent, extent, slot + 1


def kernel(n_samp, n_feat, *refs):
    (a_ref, b_ref, x_ref, u_ref, y_ref, v_ref, nx_ref, nu_ref, ny_ref, nv_ref,
     q_ref, p_ref, sbuf, srec, sout, fbuf, frec, fout, at_ref, gram_ref, g16_ref, e16_ref, map_ref,
     ahead_ref, start_ref, s_send, s_recv, f_send, f_recv) = refs
    rows, cols = a_ref.shape
    chunks = b_ref.shape[1] // LANES
    s_bits = list(range(n_samp.bit_length() - 1))
    f_bits = list(range(n_feat.bit_length() - 1))

    barrier = pltpu.get_barrier_semaphore()
    for axis, bits in (("samp", s_bits), ("feat", f_bits)):
        index = lax.axis_index(axis)
        for bit in bits:
            side = (index // (1 << bit)) % 2
            pl.semaphore_signal(
                barrier,
                inc=1,
                device_id={axis: index + (1 - 2 * side) * (1 << bit)},
                device_id_type=pl.DeviceIdType.MESH,
            )

    lanes = [slice(c * LANES, (c + 1) * LANES) for c in range(chunks)]
    for c in range(chunks):
        q = x_ref[:, lanes[c]] + u_ref[:, lanes[c]]
        q_ref[c] = q
        sbuf[0, c] = q
        p = y_ref[:, lanes[c]] + v_ref[:, lanes[c]]
        p_ref[c] = p
        fbuf[0, c] = p
    pl.semaphore_wait(barrier, len(s_bits) + len(f_bits))

    def samp_unit(it, c, h):
        n = cols // HALVES
        return all_reduce(
            sbuf.at[it, c], srec.at[it, c], sout.at[it, c], s_send.at[it, c, h], s_recv.at[it, c, h],
            "samp", s_bits, h * n, n,
        )

    def feat_unit(it, c):
        return all_reduce(
            fbuf.at[it, c], frec.at[it, c], fout.at[it, c], f_send.at[it, c], f_recv.at[it, c],
            "feat", f_bits, 0, rows,
        )

    state = {}

    def blocks(lo, hi, body):
        def step(i, carry):
            body(pl.multiple_of(i * BLOCK, BLOCK))
            return carry

        lax.fori_loop(lo, hi, step, 0)

    def gram_block(i):
        part = a_ref[pl.ds(i, BLOCK), :]
        g = lax.dot_general(part, a_ref[...], (((1,), (1,)), ((), ())), preferred_element_type=f32)
        gram_ref[pl.ds(i, BLOCK), :] = g
        g16_ref[pl.ds(i, BLOCK), :] = g.astype(bf16)

    def diagonal(i):
        row = lax.broadcasted_iota(jnp.int32, (BLOCK, rows), 0) + i
        col = lax.broadcasted_iota(jnp.int32, (BLOCK, rows), 1)
        return row == col

    def scales():
        total = jnp.zeros((1, cols), f32)
        for i in range(0, rows, BLOCK):
            part = a_ref[i:i + BLOCK, :].astype(f32)
            total = total + jnp.sum(part * part, axis=0, keepdims=True)
        factor = 1.0 / (1.0 + 2.0 * jnp.sum(total, axis=1, keepdims=True) / rows)
        state["a"] = 2.0 * factor - factor * factor
        state["b"] = factor * factor

    def flip():
        for i in range(0, rows, BLOCK):
            at_ref[:, i:i + BLOCK] = a_ref[i:i + BLOCK, :].T

    def inner_block(i):
        a, b = state["a"], state["b"]
        square = dot(g16_ref[pl.ds(i, BLOCK), :], g16_ref[...])
        inner = (b - a) * gram_ref[pl.ds(i, BLOCK), :] + b * square
        gram_ref[pl.ds(i, BLOCK), :] = inner
        e16_ref[pl.ds(i, BLOCK), :] = (inner + jnp.where(diagonal(i), 2.0 - a, 0.0)).astype(bf16)

    def rest_block(i):
        a, b = state["a"], state["b"]
        gram_ref[pl.ds(i, BLOCK), :] = a * gram_ref[pl.ds(i, BLOCK), :] - b * dot(
            g16_ref[pl.ds(i, BLOCK), :], e16_ref[...]
        )

    def map_block(i):
        a = state["a"]
        part = at_ref[pl.ds(i, BLOCK), :]
        made = a * (2.0 - a) * part.astype(f32) + dot(part, e16_ref[...])
        map_ref[pl.ds(i, BLOCK), :] = made.astype(bf16)

    def narrow():
        e16_ref[...] = gram_ref[...].astype(bf16)

    n_blocks = rows // BLOCK
    c_blocks = cols // BLOCK
    tasks = [scales, flip]
    for body, count in ((gram_block, n_blocks), (inner_block, n_blocks), (rest_block, n_blocks), (None, 0), (map_block, c_blocks)):
        if body is None:
            tasks.append(narrow)
            continue
        middle = count // 2
        tasks.append(lambda body=body, middle=middle: blocks(0, middle, body))
        tasks.append(lambda body=body, middle=middle, count=count: blocks(middle, count, body))

    def spare():
        if tasks:
            tasks.pop(0)()

    def local(it, c):
        last = it == ITERS - 1
        cons = soft_shrink(sout[it, c] * (1.0 / n_samp))
        dual = q_ref[c] - cons
        start = cons - dual
        if last:
            nu_ref[:, lanes[c]] = dual
            start_ref[c] = start
        else:
            q_ref[c] = cons
        total = fout[it, c]
        goal = b_ref[:, lanes[c]]
        corr = (goal + huber_prox(total - goal, float(n_feat)) - total) * (1.0 / n_feat)
        if last:
            nv_ref[:, lanes[c]] = -corr
        ahead = dot(a_ref[...], start.astype(bf16))
        ahead_ref[c] = ahead
        residual = ahead - (p_ref[c] + 2.0 * corr)
        if not last:
            p_ref[c] = corr
        back = joined_halves(dot(map_ref[...], split(residual)))
        if last:
            nx_ref[:, lanes[c]] = start_ref[c] - back
        else:
            q = q_ref[c] - back
            q_ref[c] = q
            sbuf[it + 1, c] = q
        yield
        partials = ahead_ref[c] - joined_halves(dot(a_ref[...], split(back)))
        if last:
            ny_ref[:, lanes[c]] = partials
        else:
            p = partials - p_ref[c]
            p_ref[c] = p
            fbuf[it + 1, c] = p
        yield

    active = []
    turn = 0

    def launch(it, c, kind, first):
        if kind == "samp":
            for h in range(HALVES):
                gen = samp_unit(it, c, h)
                next(gen)
                active.append([first + h, gen, it, c])
        else:
            gen = feat_unit(it, c)
            next(gen)
            active.append([first, gen, it, c])

    for c in range(chunks):
        launch(0, c, "feat", c * HALVES)
        launch(0, c, "samp", c * HALVES)
    done = set()
    while active:
        turn += 1
        finished = []
        for unit in list(active):
            if unit[0] < turn:
                spare()
                if next(unit[1], "end") == "end":
                    active.remove(unit)
                    finished.append((unit[2], unit[3]))
        for it, c in sorted(set(finished)):
            if any(unit[2] == it and unit[3] == c for unit in active):
                continue
            while tasks:
                spare()
            step = local(it, c)
            next(step)
            if it + 1 < ITERS:
                launch(it + 1, c, "samp", turn)
            next(step)
            if it + 1 < ITERS:
                launch(it + 1, c, "feat", turn)


def shards(n_samp, n_feat, data, targets, tile_x, x_dual, tile_y, y_dual):
    rows, cols = data.shape
    width = targets.shape[1]
    chunks = width // LANES
    s_slots = 2 * (n_samp.bit_length() - 1) - 1
    f_slots = 2 * (n_feat.bit_length() - 1) - 1
    vmem = pl.BlockSpec(memory_space=pltpu.VMEM)
    outs = pl.pallas_call(
        lambda *refs: kernel(n_samp, n_feat, *refs),
        out_shape=(
            jax.ShapeDtypeStruct((cols, width), f32),
            jax.ShapeDtypeStruct((cols, width), f32),
            jax.ShapeDtypeStruct((rows, width), f32),
            jax.ShapeDtypeStruct((rows, width), f32),
        ),
        in_specs=[vmem] * 6,
        out_specs=(vmem,) * 4,
        scratch_shapes=[
            pltpu.VMEM((chunks, cols, LANES), f32),
            pltpu.VMEM((chunks, rows, LANES), f32),
            pltpu.VMEM((ITERS, chunks, cols, LANES), f32),
            pltpu.VMEM((ITERS, chunks, cols, LANES), f32),
            pltpu.VMEM((ITERS, chunks, cols, LANES), f32),
            pltpu.VMEM((ITERS, chunks, rows, LANES), f32),
            pltpu.VMEM((ITERS, chunks, rows, LANES), f32),
            pltpu.VMEM((ITERS, chunks, rows, LANES), f32),
            pltpu.VMEM((cols, rows), bf16),
            pltpu.VMEM((rows, rows), f32),
            pltpu.VMEM((rows, rows), bf16),
            pltpu.VMEM((rows, rows), bf16),
            pltpu.VMEM((cols, rows), bf16),
            pltpu.VMEM((chunks, rows, LANES), f32),
            pltpu.VMEM((chunks, cols, LANES), f32),
            pltpu.SemaphoreType.DMA((ITERS, chunks, HALVES, s_slots)),
            pltpu.SemaphoreType.DMA((ITERS, chunks, HALVES, s_slots)),
            pltpu.SemaphoreType.DMA((ITERS, chunks, f_slots)),
            pltpu.SemaphoreType.DMA((ITERS, chunks, f_slots)),
        ],
        compiler_params=pltpu.CompilerParams(
            collective_id=0, has_side_effects=True, vmem_limit_bytes=60 * 1024 * 1024
        ),
    )(data, targets, tile_x[0], x_dual[0], tile_y[0], y_dual[0])
    return tuple(out[None] for out in outs)


def solution(mesh):
    n_samp, n_feat = mesh.shape["samp"], mesh.shape["feat"]
    return jax.shard_map(
        lambda *args: shards(n_samp, n_feat, *args),
        mesh=mesh,
        in_specs=(
            P("samp", "feat"),
            P("samp", None),
            P("samp", "feat", None),
            P("samp", "feat", None),
            P("feat", "samp", None),
            P("feat", "samp", None),
        ),
        out_specs=(
            P("samp", "feat", None),
            P("samp", "feat", None),
            P("feat", "samp", None),
            P("feat", "samp", None),
        ),
        check_vma=False,
    )
```

```python
import jax
import jax.numpy as jnp
from jax import lax
from jax.experimental import pallas as pl
from jax.experimental.pallas import tpu as pltpu
from jax.sharding import PartitionSpec as P

ITERS = 2
LANES = 128
BLOCK = 256
PIECES = 4
huber_width = 0.5
shrink_level = 0.1
f32 = jnp.float32
bf16 = jnp.bfloat16


def dot(a, b):
    return jnp.dot(a, b, preferred_element_type=f32)


def split(value):
    high = value.astype(bf16)
    low = (value - high.astype(f32)).astype(bf16)
    return jnp.concatenate([high, low], axis=1)


def joined_halves(value):
    return value[:, :LANES] + value[:, LANES:]


def soft_shrink(values):
    return values - jnp.clip(values, -shrink_level, shrink_level)


def huber_prox(values, weight):
    limit = huber_width * (1.0 + weight)
    shift = jnp.where(values > 0.0, weight * huber_width, -weight * huber_width)
    return jnp.where(jnp.abs(values) <= limit, values * (1.0 / (1.0 + weight)), values - shift)


def all_reduce(buf, rec, out, send, recv, axis, order, base, rows):
    index = lax.axis_index(axis)
    off, length, at, slot = base, rows, base, 0
    path = []
    for k, bit in enumerate(order):
        side = (index // (1 << bit)) % 2
        peer = index + (1 - 2 * side) * (1 << bit)
        if k < len(order) - 1:
            half = length // 2
            keep = off + side * half
            give = off + (1 - side) * half
            path.append((peer, off, length))
        else:
            half, keep, give = length, off, off
        if not isinstance(keep, int):
            keep, give = pl.multiple_of(keep, 8), pl.multiple_of(give, 8)
        copy = pltpu.make_async_remote_copy(
            src_ref=buf.at[pl.ds(give, half)],
            dst_ref=rec.at[pl.ds(at, half)],
            send_sem=send.at[slot],
            recv_sem=recv.at[slot],
            device_id={axis: peer},
            device_id_type=pl.DeviceIdType.MESH,
        )
        copy.start()
        yield
        copy.wait()
        target = buf if k < len(order) - 1 else out
        target[pl.ds(keep, half)] = buf[pl.ds(keep, half)] + rec[pl.ds(at, half)]
        off, length, at, slot = keep, half, at + half, slot + 1
    for peer, parent, extent in reversed(path):
        copy = pltpu.make_async_remote_copy(
            src_ref=out.at[pl.ds(off, length)],
            dst_ref=out.at[pl.ds(off, length)],
            send_sem=send.at[slot],
            recv_sem=recv.at[slot],
            device_id={axis: peer},
            device_id_type=pl.DeviceIdType.MESH,
        )
        copy.start()
        yield
        copy.wait()
        off, length, slot = parent, extent, slot + 1


def kernel(n_samp, n_feat, *refs):
    (a_ref, b_ref, x_ref, u_ref, y_ref, v_ref, nx_ref, nu_ref, ny_ref, nv_ref,
     q_ref, p_ref, sbuf, srec, sout, fbuf, frec, fout, at_ref, gram_ref, g16_ref, e16_ref, map_ref,
     ahead_ref, start_ref, s_send, s_recv, f_send, f_recv) = refs
    rows, cols = a_ref.shape
    chunks = b_ref.shape[1] // LANES
    s_bits = list(range(n_samp.bit_length() - 1))
    s_turned = s_bits[1:2] + s_bits[:1] + s_bits[2:]
    f_bits = list(range(n_feat.bit_length() - 1))

    barrier = pltpu.get_barrier_semaphore()
    for axis, bits in (("samp", s_bits), ("feat", f_bits)):
        index = lax.axis_index(axis)
        for bit in bits:
            side = (index // (1 << bit)) % 2
            pl.semaphore_signal(
                barrier,
                inc=1,
                device_id={axis: index + (1 - 2 * side) * (1 << bit)},
                device_id_type=pl.DeviceIdType.MESH,
            )

    lanes = [slice(c * LANES, (c + 1) * LANES) for c in range(chunks)]
    for c in range(chunks):
        q = x_ref[:, lanes[c]] + u_ref[:, lanes[c]]
        q_ref[c] = q
        sbuf[0, c] = q
        p = y_ref[:, lanes[c]] + v_ref[:, lanes[c]]
        p_ref[c] = p
        fbuf[0, c] = p
    pl.semaphore_wait(barrier, len(s_bits) + len(f_bits))

    def samp_unit(it, c, h):
        n = cols // PIECES
        return all_reduce(
            sbuf.at[it, c], srec.at[it, c], sout.at[it, c], s_send.at[it, c, h], s_recv.at[it, c, h],
            "samp", s_turned if h == 0 else s_bits, h * n, n,
        )

    def feat_unit(it, c):
        return all_reduce(
            fbuf.at[it, c], frec.at[it, c], fout.at[it, c], f_send.at[it, c], f_recv.at[it, c],
            "feat", f_bits, 0, rows,
        )

    state = {}

    def blocks(lo, hi, body):
        def step(i, carry):
            body(pl.multiple_of(i * BLOCK, BLOCK))
            return carry

        lax.fori_loop(lo, hi, step, 0)

    def gram_block(i):
        part = a_ref[pl.ds(i, BLOCK), :]
        g = lax.dot_general(part, a_ref[...], (((1,), (1,)), ((), ())), preferred_element_type=f32)
        gram_ref[pl.ds(i, BLOCK), :] = g
        g16_ref[pl.ds(i, BLOCK), :] = g.astype(bf16)

    def diagonal(i):
        row = lax.broadcasted_iota(jnp.int32, (BLOCK, rows), 0) + i
        col = lax.broadcasted_iota(jnp.int32, (BLOCK, rows), 1)
        return row == col

    def scales():
        total = jnp.zeros((1, cols), f32)
        for i in range(0, rows, BLOCK):
            part = a_ref[i:i + BLOCK, :].astype(f32)
            total = total + jnp.sum(part * part, axis=0, keepdims=True)
        factor = 1.0 / (1.0 + 2.0 * jnp.sum(total, axis=1, keepdims=True) / rows)
        state["a"] = 2.0 * factor - factor * factor
        state["b"] = factor * factor

    def flip():
        for i in range(0, rows, BLOCK):
            at_ref[:, i:i + BLOCK] = a_ref[i:i + BLOCK, :].T

    def inner_block(i):
        a, b = state["a"], state["b"]
        square = dot(g16_ref[pl.ds(i, BLOCK), :], g16_ref[...])
        inner = (b - a) * gram_ref[pl.ds(i, BLOCK), :] + b * square
        gram_ref[pl.ds(i, BLOCK), :] = inner
        e16_ref[pl.ds(i, BLOCK), :] = (inner + jnp.where(diagonal(i), 2.0 - a, 0.0)).astype(bf16)

    def rest_block(i):
        a, b = state["a"], state["b"]
        gram_ref[pl.ds(i, BLOCK), :] = a * gram_ref[pl.ds(i, BLOCK), :] - b * dot(
            g16_ref[pl.ds(i, BLOCK), :], e16_ref[...]
        )

    def map_block(i):
        a = state["a"]
        part = at_ref[pl.ds(i, BLOCK), :]
        made = a * (2.0 - a) * part.astype(f32) + dot(part, e16_ref[...])
        map_ref[pl.ds(i, BLOCK), :] = made.astype(bf16)

    def narrow():
        e16_ref[...] = gram_ref[...].astype(bf16)

    n_blocks = rows // BLOCK
    c_blocks = cols // BLOCK
    tasks = [scales, flip]
    for body, count in ((gram_block, n_blocks), (inner_block, n_blocks), (rest_block, n_blocks), (None, 0), (map_block, c_blocks)):
        if body is None:
            tasks.append(narrow)
            continue
        middle = count // 2
        tasks.append(lambda body=body, middle=middle: blocks(0, middle, body))
        tasks.append(lambda body=body, middle=middle, count=count: blocks(middle, count, body))

    def spare():
        if tasks:
            tasks.pop(0)()

    def local(it, c):
        last = it == ITERS - 1
        cons = soft_shrink(sout[it, c] * (1.0 / n_samp))
        dual = q_ref[c] - cons
        start = cons - dual
        if last:
            nu_ref[:, lanes[c]] = dual
            start_ref[c] = start
        else:
            q_ref[c] = cons
        total = fout[it, c]
        goal = b_ref[:, lanes[c]]
        corr = (goal + huber_prox(total - goal, float(n_feat)) - total) * (1.0 / n_feat)
        if last:
            nv_ref[:, lanes[c]] = -corr
        ahead = dot(a_ref[...], start.astype(bf16))
        ahead_ref[c] = ahead
        residual = ahead - (p_ref[c] + 2.0 * corr)
        if not last:
            p_ref[c] = corr
        yield None
        back = joined_halves(dot(map_ref[...], split(residual)))
        if last:
            nx_ref[:, lanes[c]] = start_ref[c] - back
        else:
            q = q_ref[c] - back
            q_ref[c] = q
            sbuf[it + 1, c] = q
        yield None if last else "samp"
        partials = ahead_ref[c] - joined_halves(dot(a_ref[...], split(back)))
        if last:
            ny_ref[:, lanes[c]] = partials
        else:
            p = partials - p_ref[c]
            p_ref[c] = p
            fbuf[it + 1, c] = p
        yield None if last else "feat"

    active = []
    turn = 0

    def launch(it, c, kind, first):
        if kind == "samp":
            for h in range(PIECES):
                gen = samp_unit(it, c, h)
                next(gen)
                active.append([first + h, gen, it, c])
        else:
            gen = feat_unit(it, c)
            next(gen)
            active.append([first, gen, it, c])

    for c in range(chunks):
        launch(0, c, "feat", c * PIECES)
        launch(0, c, "samp", c * PIECES)
    working = []
    count = 0
    while active or working:
        turn += 1
        finished = set()
        for unit in list(active):
            if unit[0] < turn:
                count += 1
                if count % 2 == 0:
                    spare()
                if next(unit[1], "end") == "end":
                    active.remove(unit)
                    finished.add((unit[2], unit[3]))
        for work in list(working):
            it, c, step = work
            kind = next(step, "end")
            if kind == "end":
                working.remove(work)
            elif kind is not None:
                launch(it + 1, c, kind, turn)
        for it, c in sorted(finished):
            if any(unit[2] == it and unit[3] == c for unit in active):
                continue
            while tasks:
                spare()
            step = local(it, c)
            next(step)
            working.append((it, c, step))


def shards(n_samp, n_feat, data, targets, tile_x, x_dual, tile_y, y_dual):
    rows, cols = data.shape
    width = targets.shape[1]
    chunks = width // LANES
    s_slots = 2 * (n_samp.bit_length() - 1) - 1
    f_slots = 2 * (n_feat.bit_length() - 1) - 1
    vmem = pl.BlockSpec(memory_space=pltpu.VMEM)
    outs = pl.pallas_call(
        lambda *refs: kernel(n_samp, n_feat, *refs),
        out_shape=(
            jax.ShapeDtypeStruct((cols, width), f32),
            jax.ShapeDtypeStruct((cols, width), f32),
            jax.ShapeDtypeStruct((rows, width), f32),
            jax.ShapeDtypeStruct((rows, width), f32),
        ),
        in_specs=[vmem] * 6,
        out_specs=(vmem,) * 4,
        scratch_shapes=[
            pltpu.VMEM((chunks, cols, LANES), f32),
            pltpu.VMEM((chunks, rows, LANES), f32),
            pltpu.VMEM((ITERS, chunks, cols, LANES), f32),
            pltpu.VMEM((ITERS, chunks, cols, LANES), f32),
            pltpu.VMEM((ITERS, chunks, cols, LANES), f32),
            pltpu.VMEM((ITERS, chunks, rows, LANES), f32),
            pltpu.VMEM((ITERS, chunks, rows, LANES), f32),
            pltpu.VMEM((ITERS, chunks, rows, LANES), f32),
            pltpu.VMEM((cols, rows), bf16),
            pltpu.VMEM((rows, rows), f32),
            pltpu.VMEM((rows, rows), bf16),
            pltpu.VMEM((rows, rows), bf16),
            pltpu.VMEM((cols, rows), bf16),
            pltpu.VMEM((chunks, rows, LANES), f32),
            pltpu.VMEM((chunks, cols, LANES), f32),
            pltpu.SemaphoreType.DMA((ITERS, chunks, PIECES, s_slots)),
            pltpu.SemaphoreType.DMA((ITERS, chunks, PIECES, s_slots)),
            pltpu.SemaphoreType.DMA((ITERS, chunks, f_slots)),
            pltpu.SemaphoreType.DMA((ITERS, chunks, f_slots)),
        ],
        compiler_params=pltpu.CompilerParams(
            collective_id=0, has_side_effects=True, vmem_limit_bytes=60 * 1024 * 1024
        ),
    )(data, targets, tile_x[0], x_dual[0], tile_y[0], y_dual[0])
    return tuple(out[None] for out in outs)


def solution(mesh):
    n_samp, n_feat = mesh.shape["samp"], mesh.shape["feat"]
    return jax.shard_map(
        lambda *args: shards(n_samp, n_feat, *args),
        mesh=mesh,
        in_specs=(
            P("samp", "feat"),
            P("samp", None),
            P("samp", "feat", None),
            P("samp", "feat", None),
            P("feat", "samp", None),
            P("feat", "samp", None),
        ),
        out_specs=(
            P("samp", "feat", None),
            P("samp", "feat", None),
            P("feat", "samp", None),
            P("feat", "samp", None),
        ),
        check_vma=False,
    )
```
